32 devices in a mesh: parts: 2 (over x), ctx: 16 (over z, y, core).
Axes of the slice: x: 2, y: 2, z: 4, core: 2. Of those that a mesh axis runs over, the one named last changes fastest.
Arguments:
- query_rows: bfloat16 [2, 4096, 1536], P(None, ('parts', 'ctx')), parts along dimension 1, may hold values from -6 to 6
- key_rows: bfloat16 [2, 4096, 1536], P(None, ('parts', 'ctx')), parts along dimension 1, may hold values from -4 to 4
- value_rows: bfloat16 [2, 4096, 1536], P(None, ('parts', 'ctx')), parts along dimension 1, may hold values from -12 to 12
- step_rates: float32 [2, 4096, 4], P(None, ('parts', 'ctx')), parts along dimension 1, may hold values from 0.01 to 1
- gate_weight: float32 [3072, 384], P(('parts', 'ctx')), parts along dimension 0, may hold values from -0.3125 to 0.3125
- up_weight: float32 [3072, 384], P(('parts', 'ctx')), parts along dimension 0, may hold values from -0.3125 to 0.3125
- down_weight: float32 [3072, 384], P(('parts', 'ctx')), parts along dimension 0, may hold values from -0.3125 to 0.3125
Outputs:
- attended: bfloat16 [2, 4096, 1536], P(None, ('parts', 'ctx')), parts along dimension 1
- gate_next: float32 [3072, 384], P(('parts', 'ctx')), parts along dimension 0
- up_next: float32 [3072, 384], P(('parts', 'ctx')), parts along dimension 0
- down_next: float32 [3072, 384], P(('parts', 'ctx')), parts along dimension 0
The draws below stay inside these ranges and needn't reach their ends.
There are 2 independent parts, one for each index of `parts`. The reference program is written for one: setup_inputs(seed, part) draws one part's arguments, and reference() takes and returns one part's arrays. A program takes and returns all parts, laid end to end along the dimension named above; each array names one. Nothing has to cross between parts.
All inputs are finite; a program needn't handle non-finite values.
Results may differ from the reference program's by a relative error of at most 0.0081.
Values may be sent and summed in bfloat16 or wider, within the bound.
No kernel may reach another device: no remote copies, remote signals or barrier semaphores. Data moves between devices by JAX's collectives and lax.ppermute only.
A program may use at most 64 MiB of HBM per device.

```python
import math
import jax
import jax.numpy as jnp
from jax import lax

H = 4
DH = 384
FH = 384
SPANS = 2
TOK_DEV = 128
TOKENS = 2048
HD = 1536
HF = 1536


def token_fields(key):
    shape = (SPANS, TOKENS, HD)
    key_base = jax.random.fold_in(key, 101)
    value_base = jax.random.fold_in(key, 202)
    pairing_base = jax.random.fold_in(key, 404)
    key_noise = jax.random.truncated_normal(key_base, -4.0, 4.0, shape, jnp.float32)
    value_noise = jax.random.truncated_normal(value_base, -4.0, 4.0, shape, jnp.float32)
    blocks = TOKENS // TOK_DEV
    pairing = jax.random.permutation(pairing_base, blocks)
    token_block = jnp.arange(TOKENS, dtype=jnp.int32) // TOK_DEV
    feature_block = jnp.arange(HD, dtype=jnp.int32) // (HD // blocks)
    boosted = jnp.where(pairing[token_block][:, None] == feature_block[None, :], 5.0, 1.0).astype(jnp.float32)
    keys_drawn = key_noise
    values_drawn = 0.9 * key_noise + 0.44 * boosted[None, :, :] * value_noise
    return (keys_drawn, jnp.clip(values_drawn, -12.0, 12.0))


def draw_key_rows(key, part):
    return token_fields(key)[0].astype(jnp.bfloat16)


def draw_value_rows(key, part):
    return token_fields(key)[1].astype(jnp.bfloat16)


def level_of(own_key, extent, cuts, smallest, largest):
    factor_of = 1.0
    for axis_at, parts in cuts:
        heights = jax.random.uniform(jax.random.fold_in(jax.random.fold_in(own_key, 6), axis_at), (parts,), jnp.float32, smallest / len(cuts), largest / len(cuts))
        factor_of = factor_of * jnp.repeat(jnp.exp(heights), extent[axis_at] // parts).reshape((-1,) + (1,) * (len(extent) - 1 - axis_at))
    return factor_of


def noise(own_key, dims, spread, limit, shards=(), kind=jnp.bfloat16):
    factor_of = level_of(own_key, dims, shards, -0.22, 0.18) if shards else 1.0
    result = jax.random.normal(own_key, dims, jnp.float32) * spread * factor_of
    return jnp.minimum(jnp.maximum(result, -limit), limit).astype(kind)


def setup_inputs(seed: int = 0, part: int = 0) -> dict:
    seeds = jax.random.split(jax.random.key(seed), 8)
    own_keys = jax.random.split(jax.random.fold_in(seeds[7], part), 8)
    query_rows = noise(own_keys[0], (SPANS, TOKENS, HD), 1.0, 6.0, ((1, 16),))
    key_rows = draw_key_rows(jax.random.fold_in(jax.random.fold_in(seeds[7], part), 71), part)
    value_rows = draw_value_rows(jax.random.fold_in(jax.random.fold_in(seeds[7], part), 71), part)
    step_rates = jnp.clip(jnp.exp(math.log(1.0) - 4.6051702 * jax.random.uniform(own_keys[3], (SPANS, TOKENS, H), jnp.float32) ** level_of(own_keys[3], (SPANS, TOKENS, H), ((1, 16),), -0.2, 0.2)), 0.01, 1.0)
    gate_weight = noise(own_keys[4], (HF, DH), DH ** -0.5, 0.3125, ((0, 16),), jnp.float32)
    up_weight = noise(own_keys[5], (HF, DH), DH ** -0.5, 0.3125, ((0, 16),), jnp.float32)
    down_weight = noise(own_keys[6], (HD, FH), FH ** -0.5, 0.3125, ((0, 16),), jnp.float32)
    return {"query_rows": query_rows, "key_rows": key_rows, "value_rows": value_rows, "step_rates": step_rates, "gate_weight": gate_weight, "up_weight": up_weight, "down_weight": down_weight}


def silu_parts(values):
    sig = jax.nn.sigmoid(values)
    return (values * sig, sig * (1.0 + values * (1.0 - sig)))

def span_pass(queries, keys_here, values_here, rates, gate_low, up_low, down_low, heads):
    count = queries.shape[0]
    width = gate_low.shape[1]
    hidden = gate_low.shape[0] // heads
    gate_three = gate_low.astype(jnp.float32).reshape(heads, hidden, width)
    up_three = up_low.astype(jnp.float32).reshape(heads, hidden, width)
    down_three = down_low.astype(jnp.float32).reshape(heads, width, hidden)
    key_three = keys_here.astype(jnp.float32).reshape(count, heads, width)
    first = jnp.einsum('thd,hfd->thf', key_three, gate_three)
    second = jnp.einsum('thd,hfd->thf', key_three, up_three)
    silu_first, slope = silu_parts(first)
    acts = (silu_first * second).astype(jnp.bfloat16)
    scaled = (rates[:, :, None] * values_here.astype(jnp.float32).reshape(count, heads, width)).astype(jnp.bfloat16)
    back = jnp.einsum('thd,hdf->thf', scaled.astype(jnp.float32), down_three)
    d_gate = (back * second * slope).astype(jnp.bfloat16)
    d_up = (back * silu_first).astype(jnp.bfloat16)
    grad_gate = jnp.einsum('thf,thd->hfd', d_gate.astype(jnp.float32), key_three).reshape(heads * hidden, width)
    grad_up = jnp.einsum('thf,thd->hfd', d_up.astype(jnp.float32), key_three).reshape(heads * hidden, width)
    grad_down = jnp.einsum('thd,thf->hdf', scaled.astype(jnp.float32), acts.astype(jnp.float32)).reshape(heads * width, hidden)
    query_three = queries.astype(jnp.float32).reshape(count, heads, width)
    query_gate = jnp.einsum('thd,hfd->thf', query_three, gate_three)
    query_up = jnp.einsum('thd,hfd->thf', query_three, up_three)
    query_acts = (jax.nn.silu(query_gate) * query_up).astype(jnp.bfloat16)
    output = jnp.einsum('thf,hdf->thd', query_acts.astype(jnp.float32), down_three)
    return (output.reshape(count, heads * width).astype(jnp.bfloat16), (grad_gate, grad_up, grad_down))

def refresh(matrix, gradient, heads):
    total_rows, columns = matrix.shape
    grad_three = gradient.reshape(heads, total_rows // heads, columns)
    block_mean = lax.optimization_barrier(jnp.mean(grad_three * grad_three, axis=(1, 2)))
    factor = lax.rsqrt(block_mean + 1e-06) / math.sqrt(columns)
    stepped = matrix + (grad_three * factor[:, None, None]).reshape(total_rows, columns)
    row_mean = lax.optimization_barrier(jnp.mean(stepped * stepped, axis=1, keepdims=True))
    return stepped * lax.rsqrt(row_mean + 1e-06) / math.sqrt(columns)

def reference(query_rows, key_rows, value_rows, step_rates, gate_weight, up_weight, down_weight):
    heads = step_rates.shape[2]
    masters = (gate_weight, up_weight, down_weight)
    results = []
    for span_index in range(SPANS):
        lowered = tuple((matrix.astype(jnp.bfloat16) for matrix in masters))
        output, grads = span_pass(query_rows[span_index], key_rows[span_index], value_rows[span_index], step_rates[span_index], lowered[0], lowered[1], lowered[2], heads)
        results.append(output)
        masters = tuple((refresh(masters[i], grads[i], heads) for i in range(3)))
    return (jnp.stack(results), masters[0], masters[1], masters[2])
```

```python
import math

import jax
import jax.numpy as jnp
from jax import lax
from jax.sharding import PartitionSpec as P


def swap(value, mask):
    pairs = [(source, source ^ mask) for source in range(lax.axis_size("ctx"))]
    return lax.ppermute(value, "ctx", pairs)


def silu_parts(values):
    sig = jax.nn.sigmoid(values)
    return (values * sig, sig * (1.0 + values * (1.0 - sig)))


def mul(a, b, contract):
    return lax.dot_general(a, b, ((contract[0:1], contract[1:2]), ((), ())), preferred_element_type=jnp.float32)


def gradients(keys, scaled, low):
    gate, up, down = low
    first = mul(keys, gate, (1, 1))
    second = mul(keys, up, (1, 1))
    silu_first, slope = silu_parts(first)
    acts = (silu_first * second).astype(jnp.bfloat16)
    back = mul(scaled, down, (1, 0))
    d_gate = (back * second * slope).astype(jnp.bfloat16)
    d_up = (back * silu_first).astype(jnp.bfloat16)
    return jnp.stack([mul(d_gate, keys, (0, 0)), mul(d_up, keys, (0, 0)), mul(scaled, acts, (0, 0))])


def answers(queries, low):
    gate, up, down = low
    acts = (jax.nn.silu(mul(queries, gate, (1, 1))) * mul(queries, up, (1, 1))).astype(jnp.bfloat16)
    return mul(acts, down, (1, 1)).astype(jnp.bfloat16)


def pick(array, axis, index):
    return lax.dynamic_index_in_dim(array, index, axis, keepdims=False)


def refreshed(masters, grads, totals, per_head):
    columns = masters.shape[2]
    factor = lax.rsqrt(totals / (per_head * columns) + 1e-06) / math.sqrt(columns)
    stepped = masters + grads * factor[:, None, None]
    row_mean = jnp.mean(stepped * stepped, axis=2, keepdims=True)
    return stepped * lax.rsqrt(row_mean + 1e-06) / math.sqrt(columns)


def per_device(query_rows, key_rows, value_rows, step_rates, gate_weight, up_weight, down_weight):
    spans, count, total_width = query_rows.shape
    heads = step_rates.shape[2]
    width = total_width // heads
    groups = lax.axis_size("ctx") // heads
    bits = groups.bit_length() - 1
    position = lax.axis_index("ctx")
    plane = position // groups
    side = [position >> level & 1 for level in range(bits)]
    shifts = sorted(range(1, heads), key=lambda m: -m.bit_length())

    def exchange(array):
        parts = [pick(array, array.ndim - 2, plane)]
        for shift in shifts:
            parts.append(swap(pick(array, array.ndim - 2, plane ^ shift), shift * groups))
        return parts

    keys = key_rows.reshape(spans, count, heads, width)
    queries = query_rows.reshape(spans, count, heads, width)
    values = value_rows.reshape(spans, count, heads, width).astype(jnp.float32)
    scaled = (step_rates[:, :, :, None] * values).astype(jnp.bfloat16)

    masters = jnp.stack([gate_weight, up_weight, down_weight])
    rows = masters.shape[1]
    pairs = [exchange(jnp.stack([keys[c], scaled[c]])) for c in range(spans)]
    asked = [exchange(queries[c]) for c in range(spans)]

    whole = masters[:, None]
    for level in reversed(range(bits)):
        other = swap(whole, 1 << level)
        low_first = side[level] == 0
        both = jnp.stack([jnp.where(low_first, whole, other), jnp.where(low_first, other, whole)], axis=2)
        whole = both.reshape(3, -1, rows, width)
    whole = whole.reshape(3, groups * rows, width)

    outs = []
    for c in range(spans):
        low = whole.astype(jnp.bfloat16)
        token_keys = jnp.concatenate([part[0] for part in pairs[c]])
        token_scaled = jnp.concatenate([part[1] for part in pairs[c]])
        grads = gradients(token_keys, token_scaled, low)
        outs.append(answers(jnp.concatenate(asked[c]), low))
        last = c == spans - 1
        share = grads.reshape((3,) + (2,) * bits + (rows, width))
        stops = range(bits) if last else range(bits - 1)
        for level in stops:
            axis = bits - level
            kept = pick(share, axis, side[level])
            sent = pick(share, axis, 1 - side[level]).astype(jnp.bfloat16)
            share = kept + swap(sent, 1 << level).astype(jnp.float32)
        if last:
            totals = jnp.sum(share * share, axis=(1, 2))
            for level in range(bits):
                totals = totals + swap(totals, 1 << level)
            own = lax.dynamic_slice_in_dim(whole, (position % groups) * rows, rows, 1)
            own = refreshed(own, share, totals, groups * rows)
        else:
            top = bits - 1
            share = share + swap(share.astype(jnp.bfloat16), 1 << top).astype(jnp.float32)
            for level in reversed(range(bits - 1)):
                axis = bits - level
                other = swap(share.astype(jnp.bfloat16), 1 << level).astype(jnp.float32)
                low_first = side[level] == 0
                share = jnp.stack([jnp.where(low_first, share, other), jnp.where(low_first, other, share)], axis=axis)
            share = share.reshape(3, groups * rows, width)
            totals = jnp.sum(share * share, axis=(1, 2))
            whole = refreshed(whole, share, totals, groups * rows)

    finished = []
    for c in range(spans):
        parts = outs[c].reshape(heads, count, width)
        result = jnp.zeros((count, heads, width), jnp.bfloat16)
        result = lax.dynamic_update_index_in_dim(result, parts[0], plane, 1)
        for at, shift in enumerate(shifts):
            back = swap(parts[at + 1], shift * groups)
            result = lax.dynamic_update_index_in_dim(result, back, plane ^ shift, 1)
        finished.append(result.reshape(count, total_width))
    return (jnp.stack(finished), own[0], own[1], own[2])


def solution(mesh):
    tokens = P(None, ("parts", "ctx"), None)
    weights = P(("parts", "ctx"), None)
    return jax.shard_map(
        per_device,
        mesh=mesh,
        in_specs=(tokens,) * 4 + (weights,) * 3,
        out_specs=(tokens,) + (weights,) * 3,
        check_vma=False,
    )
```

```python
import functools
import math

import jax
import jax.numpy as jnp
from jax import lax
from jax.experimental import pallas as pl
from jax.experimental.pallas import tpu as pltpu
from jax.sharding import PartitionSpec as P


SMEM = pl.BlockSpec(memory_space=pltpu.SMEM)
VMEM = pl.BlockSpec(memory_space=pltpu.VMEM)
HBM = pl.BlockSpec(memory_space=pltpu.HBM)
F32 = jnp.float32
BF16 = jnp.bfloat16


def shape_of(shape, dtype):
    return jax.ShapeDtypeStruct(shape, dtype)


def swap(value, mask):
    pairs = [(source, source ^ mask) for source in range(lax.axis_size("ctx"))]
    return lax.ppermute(value, "ctx", pairs)


def silu_parts(values):
    sig = jax.nn.sigmoid(values)
    return (values * sig, sig * (1.0 + values * (1.0 - sig)))


def mul(a, b, left, right):
    return lax.dot_general(a, b, (((left,), (right,)), ((), ())), preferred_element_type=F32)


def columns_of(head, width):
    return pl.ds(pl.multiple_of(head * width, 128), width)


def start_all(copies):
    for copy in copies:
        copy.start()
    return copies


def pack_pairs(c, ids, key_ref, value_ref, rate_ref, *refs):
    outs, (value_s, rate_s, sems) = refs[:-3], refs[-3:]
    heads, _, width = value_s.shape
    rate_copy = pltpu.make_async_copy(rate_ref.at[c], rate_s.at[pl.ds(0, heads)], sems.at[2, 0])
    rate_copy.start()
    copies = []
    for at, out in enumerate(outs):
        cols = columns_of(ids[2 + at], width)
        copies.append(start_all((
            pltpu.make_async_copy(value_ref.at[c, :, cols], value_s.at[at], sems.at[0, at]),
            pltpu.make_async_copy(key_ref.at[c, :, cols], out.at[0], sems.at[1, at]),
        )))
    rate_copy.wait()
    rates = jnp.transpose(rate_s[...])
    lanes = lax.broadcasted_iota(jnp.int32, rates.shape, 1)
    for at, out in enumerate(outs):
        rate = jnp.sum(jnp.where(lanes == ids[2 + at], rates, 0.0), axis=1, keepdims=True)
        copies[at][0].wait()
        out[1] = (rate * value_s[at].astype(F32)).astype(BF16)
        copies[at][1].wait()


def pack_own(ids, *refs):
    masters, (own, low, sems) = refs[:-3], refs[-3:]
    loads = start_all([pltpu.make_async_copy(m, own.at[at], sems.at[at]) for at, m in enumerate(masters)])
    for at, load in enumerate(loads):
        load.wait()
        low[at] = own[at].astype(BF16)


def pack_queries(ids, query_ref, *refs):
    outs, sems = refs[:-1], refs[-1]
    heads = len(outs) - 2
    width = outs[0].shape[1]
    targets = [(1, ids[2 + at], outs[at]) for at in range(heads)]
    targets += [(0, ids[2 + at], outs[heads + at // 2].at[min(at, 3 - at)]) for at in range(heads)]
    copies = start_all([
        pltpu.make_async_copy(query_ref.at[c, :, columns_of(head, width)], out, sems.at[at])
        for at, (c, head, out) in enumerate(targets)
    ])
    for copy in copies:
        copy.wait()


def gradients(keys, scaled, gate, up, down, store):
    first = mul(keys, gate, 1, 1)
    second = mul(keys, up, 1, 1)
    silu_first, slope = silu_parts(first)
    acts = (silu_first * second).astype(BF16)
    back = mul(scaled, down, 1, 0)
    d_gate = (back * second * slope).astype(BF16)
    d_up = (back * silu_first).astype(BF16)
    store(0, mul(d_gate, keys, 0, 0))
    store(1, mul(d_up, keys, 0, 0))
    store(2, mul(scaled, acts, 0, 0))


def gather_tokens(parts, key_s, scaled_s):
    count = parts[0].shape[1]
    for at, part in enumerate(parts):
        key_s[at * count : (at + 1) * count] = part[0]
        scaled_s[at * count : (at + 1) * count] = part[1]


def quarter(top, low, rows):
    return pl.ds(pl.multiple_of((2 * top + low) * rows, 16), rows)


def spread_rows(c, y, own, top, low, both, out):
    rows = own.shape[1]
    for m in range(3):
        for yy, cc, part in ((y, c, own), (1 - y, c, top), (y, 1 - c, low), (1 - y, 1 - c, both)):
            out[m, quarter(yy, cc, rows)] = part[m].astype(BF16)


def first_step(ids, *refs):
    heads = len(refs) - 9
    parts = refs[:heads]
    own, top, low, both, low_ref, full, sent, key_s, scaled_s = refs[heads:]
    c, y = ids[0], ids[1]
    spread_rows(c, y, own, top, low, both, low_ref)
    gather_tokens(parts, key_s, scaled_s)

    def store(m, grad):
        full[m] = grad
        sent[m] = grad.astype(BF16)

    gradients(key_s[...], scaled_s[...], low_ref[0], low_ref[1], low_ref[2], store)


def half_sum(ids, full, other, out):
    c = ids[0]
    rows = out.shape[2]
    for m in range(3):
        for y in range(2):
            at = quarter(y, c, rows)
            out[m, y] = (full[m, at] + other[m, at].astype(F32)).astype(BF16)


def root_mean(values, columns):
    mean = jnp.mean(values * values, axis=1, keepdims=True)
    return values * lax.rsqrt(mean + 1e-06) / math.sqrt(columns)


def second_step(ids, *refs):
    heads = len(refs) - 16
    parts = refs[:heads]
    own, top, low, both, full, other, near, far, low_ref, mine, kept, sent, total_s, key_s, scaled_s, grad_s = refs[heads:]
    c, y = ids[0], ids[1]
    rows, columns = own.shape[1:]
    for m in range(3):
        for q in range(2):
            for cc, extra in ((c, near), (1 - c, far)):
                at = quarter(q, cc, rows)
                total_s[m, at] = full[m, at] + other[m, at].astype(F32) + extra[m, q].astype(F32)
        total = jnp.sum(jnp.sum(total_s[m] * total_s[m], axis=0, keepdims=True), axis=1, keepdims=True)
        factor = lax.rsqrt(total / (4 * rows * columns) + 1e-06) / math.sqrt(columns)
        for yy, cc, master in ((y, c, own), (1 - y, c, top), (y, 1 - c, low), (1 - y, 1 - c, both)):
            at = quarter(yy, cc, rows)
            fresh = root_mean(master[m] + total_s[m, at] * factor, columns)
            low_ref[m, at] = fresh.astype(BF16)
            if master is own:
                mine[m] = fresh
    gather_tokens(parts, key_s, scaled_s)

    def store(m, grad):
        grad_s[m] = grad
        for q in range(2):
            kept[m, q] = grad_s[m, quarter(q, c, rows)]
            sent[m, q] = grad_s[m, quarter(q, 1 - c, rows)].astype(BF16)

    gradients(key_s[...], scaled_s[...], low_ref[0], low_ref[1], low_ref[2], store)


def quarter_sum(ids, kept, other, own, sent):
    y = ids[1]
    for m in range(3):
        own[m] = kept[m, y] + other[m, y].astype(F32)
        sent[m] = (kept[m, 1 - y] + other[m, 1 - y].astype(F32)).astype(BF16)


def answers(queries, low):
    gate, up, down = low
    acts = (jax.nn.silu(mul(queries, gate, 1, 1)) * mul(queries, up, 1, 1)).astype(BF16)
    return mul(acts, down, 1, 1).astype(BF16)


def answer_one(ids, *refs):
    heads = (len(refs) - 2) // 2
    parts, low, outs, query_s = refs[:heads], refs[heads], refs[heads + 1 : -1], refs[-1]
    count = parts[0].shape[0]
    for at in range(heads):
        query_s[at * count : (at + 1) * count] = parts[at][...]
    result = answers(query_s[...], [low[m] for m in range(3)])
    for at in range(heads):
        outs[at][...] = result[at * count : (at + 1) * count]


def answer_two(ids, mine, theirs, low, own, top, lower, both, kept, sent, query_s, low_s):
    c, y = ids[0], ids[1]
    count = mine.shape[1]
    spread_rows(c, y, own, top, lower, both, low_s)
    for at, weights in enumerate((low, low_s)):
        query_s[:count] = mine[at]
        query_s[count:] = theirs[at]
        result = answers(query_s[...], [weights[m] for m in range(3)])
        kept[at] = result[:count]
        sent[at] = result[count:]


def place(ids, *refs):
    parts, out, sems = refs[:-2], refs[-2], refs[-1]
    heads = len(parts) - 2
    width = parts[0].shape[1]
    sources = [(1, ids[2 + at], parts[at]) for at in range(heads)]
    sources += [(0, ids[2 + at], parts[heads + at // 2].at[min(at, 3 - at)]) for at in range(heads)]
    copies = start_all([
        pltpu.make_async_copy(part, out.at[c, :, columns_of(head, width)], sems.at[at])
        for at, (c, head, part) in enumerate(sources)
    ])
    for copy in copies:
        copy.wait()


def finish(ids, mine, share, totals, *refs):
    outs, (fresh_s, sems) = refs[:-2], refs[-2:]
    rows, columns = mine.shape[1:]
    copies = []
    for m, out in enumerate(outs):
        factor = lax.rsqrt(totals[m, 0:1, 0:1] / (4 * rows * columns) + 1e-06) / math.sqrt(columns)
        fresh_s[m] = root_mean(mine[m] + share[m] * factor, columns)
        copies += start_all([pltpu.make_async_copy(fresh_s.at[m], out, sems.at[m])])
    for copy in copies:
        copy.wait()


def call(kernel, ids, args, outs, scratch=(), far_args=False, far_outs=False, limit=16):
    given, taken = (HBM if far else VMEM for far in (far_args, far_outs))
    space = pltpu.HBM if far_args else pltpu.VMEM
    args = [pltpu.with_memory_space_constraint(a, space) for a in args]
    if not far_outs:
        outs = jax.tree.map(lambda o: pltpu.VMEM(o.shape, o.dtype), outs)
    return pl.pallas_call(
        kernel,
        out_shape=outs,
        in_specs=[SMEM] + [given] * len(args),
        out_specs=jax.tree.map(lambda _: taken, outs),
        scratch_shapes=scratch,
        compiler_params=pltpu.CompilerParams(vmem_limit_bytes=limit << 20),
    )(ids, *args)


def fast_device(query_rows, key_rows, value_rows, step_rates, gate_weight, up_weight, down_weight):
    spans, count, total_width = query_rows.shape
    heads = step_rates.shape[2]
    width = total_width // heads
    groups = lax.axis_size("ctx") // heads
    position = lax.axis_index("ctx")
    plane = position // groups
    shifts = (2, 3, 1)
    ids = jnp.stack([position & 1, position >> 1 & 1, plane] + [plane ^ s for s in shifts]).astype(jnp.int32)
    rows = gate_weight.shape[0]
    size = groups * rows
    slab = shape_of((count, width), BF16)
    two = shape_of((2, count, width), BF16)
    whole = (3, size, width)
    half = (3, 2, rows, width)
    part = (3, rows, width)
    tokens = (pltpu.VMEM((heads * count, width), BF16),) * 2

    def pair(c):
        scratch = (
            pltpu.VMEM((heads, count, width), BF16),
            pltpu.VMEM((2 * heads, count), F32),
            pltpu.SemaphoreType.DMA((3, heads)),
        )
        arrays = (key_rows, value_rows, step_rates.transpose(0, 2, 1))
        return call(functools.partial(pack_pairs, c), ids, arrays, (two,) * heads, scratch, True)

    def spread(parts):
        return [parts[0]] + [swap(parts[at + 1], s * groups) for at, s in enumerate(shifts)]

    pairs = [spread(pair(c)) for c in range(spans)]
    own, own_low = call(
        pack_own, ids, (gate_weight, up_weight, down_weight), (shape_of(part, F32), shape_of(part, BF16)),
        (pltpu.SemaphoreType.DMA((3,)),), True,
    )
    top = swap(own, 2)
    low = swap(own, 1)
    both = swap(top, 1)
    far_own = swap(own_low, 2 * groups)
    far_top = swap(far_own, 2)
    far_low = swap(far_own, 1)
    far_both = swap(far_top, 1)
    *asked, ask_mine, ask_sent = call(
        pack_queries, ids, (query_rows,), (slab,) * heads + (two,) * 2, (pltpu.SemaphoreType.DMA((2 * heads,)),), True
    )
    asked = spread(asked)
    ask_theirs = swap(ask_sent, groups)

    weights, full, sent = call(
        first_step, ids, (*pairs[0], own, top, low, both),
        (shape_of(whole, BF16), shape_of(whole, F32), shape_of(whole, BF16)), tokens,
    )
    other = swap(sent, 1)
    near = swap(call(half_sum, ids, (full, other), shape_of(half, BF16)), 2)
    far = swap(near, 1)
    told_mine, told_sent = call(
        answer_two, ids, (ask_mine, ask_theirs, weights, far_own, far_top, far_low, far_both), (two, two),
        (pltpu.VMEM((2 * count, width), BF16), pltpu.VMEM(whole, BF16)),
    )
    told_theirs = swap(told_sent, groups)
    weights, mine, kept, sent = call(
        second_step, ids, (*pairs[1], own, top, low, both, full, other, near, far),
        (shape_of(whole, BF16), shape_of(part, F32), shape_of(half, F32), shape_of(half, BF16)),
        (pltpu.VMEM(whole, F32),) + tokens + (pltpu.VMEM(whole, F32),),
    )
    told = spread(call(answer_one, ids, (*asked, weights), (slab,) * heads, tokens[:1]))
    other = swap(sent, 1)
    share, sent = call(quarter_sum, ids, (kept, other), (shape_of(part, F32), shape_of(part, BF16)))
    share = share + swap(sent, 2).astype(F32)
    totals = jnp.broadcast_to(jnp.sum(share * share, axis=(1, 2))[:, None, None], (3, 8, 128))
    totals = totals + swap(totals, 1)
    totals = totals + swap(totals, 2)
    final = call(
        finish, ids, (mine, share, totals), (shape_of((rows, width), F32),) * 3,
        (pltpu.VMEM(part, F32), pltpu.SemaphoreType.DMA((3,))), False, True,
    )
    attended = call(
        place, ids, (*told, told_mine, told_theirs), shape_of(query_rows.shape, BF16),
        (pltpu.SemaphoreType.DMA((2 * heads,)),), False, True,
    )
    return (attended, *final)


def plain_gradients(keys, scaled, low):
    gate, up, down = low
    first = mul(keys, gate, 1, 1)
    second = mul(keys, up, 1, 1)
    silu_first, slope = silu_parts(first)
    acts = (silu_first * second).astype(jnp.bfloat16)
    back = mul(scaled, down, 1, 0)
    d_gate = (back * second * slope).astype(jnp.bfloat16)
    d_up = (back * silu_first).astype(jnp.bfloat16)
    return jnp.stack([mul(d_gate, keys, 0, 0), mul(d_up, keys, 0, 0), mul(scaled, acts, 0, 0)])


def plain_answers(queries, low):
    gate, up, down = low
    acts = (jax.nn.silu(mul(queries, gate, 1, 1)) * mul(queries, up, 1, 1)).astype(jnp.bfloat16)
    return mul(acts, down, 1, 1).astype(jnp.bfloat16)


def pick(array, axis, index):
    return lax.dynamic_index_in_dim(array, index, axis, keepdims=False)


def refreshed(masters, grads, totals, per_head):
    columns = masters.shape[2]
    factor = lax.rsqrt(totals / (per_head * columns) + 1e-06) / math.sqrt(columns)
    stepped = masters + grads * factor[:, None, None]
    row_mean = jnp.mean(stepped * stepped, axis=2, keepdims=True)
    return stepped * lax.rsqrt(row_mean + 1e-06) / math.sqrt(columns)


def plain_device(query_rows, key_rows, value_rows, step_rates, gate_weight, up_weight, down_weight):
    spans, count, total_width = query_rows.shape
    heads = step_rates.shape[2]
    width = total_width // heads
    groups = lax.axis_size("ctx") // heads
    bits = groups.bit_length() - 1
    position = lax.axis_index("ctx")
    plane = position // groups
    side = [position >> level & 1 for level in range(bits)]
    shifts = sorted(range(1, heads), key=lambda m: -m.bit_length())

    def exchange(array):
        parts = [pick(array, array.ndim - 2, plane)]
        for shift in shifts:
            parts.append(swap(pick(array, array.ndim - 2, plane ^ shift), shift * groups))
        return parts

    keys = key_rows.reshape(spans, count, heads, width)
    queries = query_rows.reshape(spans, count, heads, width)
    values = value_rows.reshape(spans, count, heads, width).astype(jnp.float32)
    scaled = (step_rates[:, :, :, None] * values).astype(jnp.bfloat16)

    masters = jnp.stack([gate_weight, up_weight, down_weight])
    rows = masters.shape[1]
    pairs = [exchange(jnp.stack([keys[c], scaled[c]])) for c in range(spans)]
    asked = [exchange(queries[c]) for c in range(spans)]

    whole = masters[:, None]
    for level in reversed(range(bits)):
        other = swap(whole, 1 << level)
        low_first = side[level] == 0
        both = jnp.stack([jnp.where(low_first, whole, other), jnp.where(low_first, other, whole)], axis=2)
        whole = both.reshape(3, -1, rows, width)
    whole = whole.reshape(3, groups * rows, width)

    outs = []
    for c in range(spans):
        low = whole.astype(jnp.bfloat16)
        token_keys = jnp.concatenate([part[0] for part in pairs[c]])
        token_scaled = jnp.concatenate([part[1] for part in pairs[c]])
        grads = plain_gradients(token_keys, token_scaled, low)
        outs.append(plain_answers(jnp.concatenate(asked[c]), low))
        last = c == spans - 1
        share = grads.reshape((3,) + (2,) * bits + (rows, width))
        stops = range(bits) if last else range(bits - 1)
        for level in stops:
            axis = bits - level
            kept = pick(share, axis, side[level])
            sent = pick(share, axis, 1 - side[level]).astype(jnp.bfloat16)
            share = kept + swap(sent, 1 << level).astype(jnp.float32)
        if last:
            totals = jnp.sum(share * share, axis=(1, 2))
            for level in range(bits):
                totals = totals + swap(totals, 1 << level)
            own = lax.dynamic_slice_in_dim(whole, (position % groups) * rows, rows, 1)
            own = refreshed(own, share, totals, groups * rows)
        else:
            top = bits - 1
            share = share + swap(share.astype(jnp.bfloat16), 1 << top).astype(jnp.float32)
            for level in reversed(range(bits - 1)):
                axis = bits - level
                other = swap(share.astype(jnp.bfloat16), 1 << level).astype(jnp.float32)
                low_first = side[level] == 0
                share = jnp.stack([jnp.where(low_first, share, other), jnp.where(low_first, other, share)], axis=axis)
            share = share.reshape(3, groups * rows, width)
            totals = jnp.sum(share * share, axis=(1, 2))
            whole = refreshed(whole, share, totals, groups * rows)

    finished = []
    for c in range(spans):
        parts = outs[c].reshape(heads, count, width)
        result = jnp.zeros((count, heads, width), jnp.bfloat16)
        result = lax.dynamic_update_index_in_dim(result, parts[0], plane, 1)
        for at, shift in enumerate(shifts):
            back = swap(parts[at + 1], shift * groups)
            result = lax.dynamic_update_index_in_dim(result, back, plane ^ shift, 1)
        finished.append(result.reshape(count, total_width))
    return (jnp.stack(finished), own[0], own[1], own[2])


def solution(mesh):
    tokens = P(None, ("parts", "ctx"), None)
    weights = P(("parts", "ctx"), None)

    def per_device(*arrays):
        heads = arrays[3].shape[2]
        rows = arrays[4].shape[0]
        fast = heads == 4 and lax.axis_size("ctx") == 16 and rows % 16 == 0
        return (fast_device if fast else plain_device)(*arrays)

    return jax.shard_map(
        per_device,
        mesh=mesh,
        in_specs=(tokens,) * 4 + (weights,) * 3,
        out_specs=(tokens,) + (weights,) * 3,
        check_vma=False,
    )
```

```python
import functools
import math

import jax
import jax.numpy as jnp
from jax import lax
from jax.experimental import pallas as pl
from jax.experimental.pallas import tpu as pltpu
from jax.sharding import PartitionSpec as P


SMEM = pl.BlockSpec(memory_space=pltpu.SMEM)
VMEM = pl.BlockSpec(memory_space=pltpu.VMEM)
HBM = pl.BlockSpec(memory_space=pltpu.HBM)
F32 = jnp.float32
BF16 = jnp.bfloat16


def shape_of(shape, dtype):
    return jax.ShapeDtypeStruct(shape, dtype)


def swap(value, mask):
    pairs = [(source, source ^ mask) for source in range(lax.axis_size("ctx"))]
    return lax.ppermute(value, "ctx", pairs)


def silu_parts(values):
    sig = jax.nn.sigmoid(values)
    return (values * sig, sig * (1.0 + values * (1.0 - sig)))


def mul(a, b, left, right):
    return lax.dot_general(a, b, (((left,), (right,)), ((), ())), preferred_element_type=F32)


def columns_of(head, width):
    return pl.ds(pl.multiple_of(head * width, 128), width)


def start_all(copies):
    for copy in copies:
        copy.start()
    return copies


def pack_pairs(c, ids, key_ref, value_ref, rate_ref, *refs):
    outs, (value_s, rate_s, sems) = refs[:-3], refs[-3:]
    heads, _, width = value_s.shape
    rate_copy = pltpu.make_async_copy(rate_ref.at[c], rate_s.at[pl.ds(0, heads)], sems.at[2, 0])
    rate_copy.start()
    copies = []
    for at, out in enumerate(outs):
        cols = columns_of(ids[2 + at], width)
        copies.append(start_all((
            pltpu.make_async_copy(value_ref.at[c, :, cols], value_s.at[at], sems.at[0, at]),
            pltpu.make_async_copy(key_ref.at[c, :, cols], out.at[0], sems.at[1, at]),
        )))
    rate_copy.wait()
    rates = jnp.transpose(rate_s[...])
    lanes = lax.broadcasted_iota(jnp.int32, rates.shape, 1)
    for at, out in enumerate(outs):
        rate = jnp.sum(jnp.where(lanes == ids[2 + at], rates, 0.0), axis=1, keepdims=True)
        copies[at][0].wait()
        out[1] = (rate * value_s[at].astype(F32)).astype(BF16)
        copies[at][1].wait()


def pack_own(ids, *refs):
    masters, (own, low, sems) = refs[:-3], refs[-3:]
    loads = start_all([pltpu.make_async_copy(m, own.at[at], sems.at[at]) for at, m in enumerate(masters)])
    for at, load in enumerate(loads):
        load.wait()
        low[at] = own[at].astype(BF16)


def slab_of(arrays, at):
    return (arrays[2].at[2], arrays[0], arrays[1], arrays[3].at[2])[at]


def pack_queries(ids, query_ref, *refs):
    outs, sems = refs[:-1], refs[-1]
    width = outs[0].shape[1]
    targets = [(1, ids[2 + at], slab_of(outs, at)) for at in range(4)]
    targets += [(0, ids[2 + at], outs[2 + at // 2].at[min(at, 3 - at)]) for at in range(4)]
    copies = start_all([
        pltpu.make_async_copy(query_ref.at[c, :, columns_of(head, width)], out, sems.at[at])
        for at, (c, head, out) in enumerate(targets)
    ])
    for copy in copies:
        copy.wait()


def gradients(keys, scaled, gate, up, down, store):
    first = mul(keys, gate, 1, 1)
    second = mul(keys, up, 1, 1)
    silu_first, slope = silu_parts(first)
    acts = (silu_first * second).astype(BF16)
    back = mul(scaled, down, 1, 0)
    d_gate = (back * second * slope).astype(BF16)
    d_up = (back * silu_first).astype(BF16)
    store(0, mul(d_gate, keys, 0, 0))
    store(1, mul(d_up, keys, 0, 0))
    store(2, mul(scaled, acts, 0, 0))


def gather_tokens(parts, key_s, scaled_s):
    count = parts[0].shape[1]
    for at, part in enumerate(parts):
        key_s[at * count : (at + 1) * count] = part[0]
        scaled_s[at * count : (at + 1) * count] = part[1]


def quarter(top, low, rows):
    return pl.ds(pl.multiple_of((2 * top + low) * rows, 16), rows)


def spread_rows(c, y, own, top, low, both, out):
    rows = own.shape[1]
    for m in range(3):
        for yy, cc, part in ((y, c, own), (1 - y, c, top), (y, 1 - c, low), (1 - y, 1 - c, both)):
            out[m, quarter(yy, cc, rows)] = part[m].astype(BF16)


def first_step(ids, *refs):
    heads = len(refs) - 9
    parts = refs[:heads]
    own, top, low, both, low_ref, full, sent, key_s, scaled_s = refs[heads:]
    c, y = ids[0], ids[1]
    spread_rows(c, y, own, top, low, both, low_ref)
    gather_tokens(parts, key_s, scaled_s)

    def store(m, grad):
        full[m] = grad
        sent[m] = grad.astype(BF16)

    gradients(key_s[...], scaled_s[...], low_ref[0], low_ref[1], low_ref[2], store)


def half_sum(ids, full, other, out):
    c = ids[0]
    rows = out.shape[2]
    for m in range(3):
        for y in range(2):
            at = quarter(y, c, rows)
            out[m, y] = (full[m, at] + other[m, at].astype(F32)).astype(BF16)


def root_mean(values, columns):
    mean = jnp.mean(values * values, axis=1, keepdims=True)
    return values * lax.rsqrt(mean + 1e-06) / math.sqrt(columns)


def renew(ids, own, top, low, both, full, other, near, far, low_ref, mine, total_s):
    c, y = ids[0], ids[1]
    rows, columns = own.shape[1:]
    for m in range(3):
        for q in range(2):
            for cc, extra in ((c, near), (1 - c, far)):
                at = quarter(q, cc, rows)
                total_s[m, at] = full[m, at] + other[m, at].astype(F32) + extra[m, q].astype(F32)
        total = jnp.sum(jnp.sum(total_s[m] * total_s[m], axis=0, keepdims=True), axis=1, keepdims=True)
        factor = lax.rsqrt(total / (4 * rows * columns) + 1e-06) / math.sqrt(columns)
        for yy, cc, master in ((y, c, own), (1 - y, c, top), (y, 1 - c, low), (1 - y, 1 - c, both)):
            at = quarter(yy, cc, rows)
            fresh = root_mean(master[m] + total_s[m, at] * factor, columns)
            low_ref[m, at] = fresh.astype(BF16)
            if master is own:
                mine[m] = fresh


def second_step(ids, *refs):
    heads = len(refs) - 6
    parts = refs[:heads]
    low, kept, sent, key_s, scaled_s, grad_s = refs[heads:]
    c = ids[0]
    rows = kept.shape[2]
    gather_tokens(parts, key_s, scaled_s)

    def store(m, grad):
        grad_s[m] = grad
        for q in range(2):
            kept[m, q] = grad_s[m, quarter(q, c, rows)]
            sent[m, q] = grad_s[m, quarter(q, 1 - c, rows)].astype(BF16)

    gradients(key_s[...], scaled_s[...], low[0], low[1], low[2], store)


def quarter_sum(ids, kept, other, own, sent):
    y = ids[1]
    for m in range(3):
        own[m] = kept[m, y] + other[m, y].astype(F32)
        sent[m] = (kept[m, 1 - y] + other[m, 1 - y].astype(F32)).astype(BF16)


def answers(queries, low):
    gate, up, down = low
    acts = (jax.nn.silu(mul(queries, gate, 1, 1)) * mul(queries, up, 1, 1)).astype(BF16)
    return mul(acts, down, 1, 1).astype(BF16)


def answer_far(ids, first, second, low, out_first, out_second, query_s):
    count = first.shape[0]
    query_s[:count] = first[...]
    query_s[count:] = second[...]
    result = answers(query_s[...], [low[m] for m in range(3)])
    out_first[...] = result[:count]
    out_second[...] = result[count:]


def answer_near(ids, mine, theirs, low, own, top, lower, both, fresh, kept, sent, query_s, low_s):
    c, y = ids[0], ids[1]
    count = mine.shape[1]
    spread_rows(c, y, own, top, lower, both, low_s)
    for at, weights in enumerate((low, low_s, fresh)):
        query_s[:count] = mine[at]
        query_s[count:] = theirs[at]
        result = answers(query_s[...], [weights[m] for m in range(3)])
        kept[at] = result[:count]
        sent[at] = result[count:]


def close(ids, mine, share, *refs):
    norms, parts = refs[:4], refs[4:8]
    out, masters, (fresh_s, sems) = refs[8], refs[9:12], refs[12:]
    width = parts[0].shape[1]
    sources = [(1, ids[2 + at], slab_of(parts, at)) for at in range(4)]
    sources += [(0, ids[2 + at], parts[2 + at // 2].at[min(at, 3 - at)]) for at in range(4)]
    copies = start_all([
        pltpu.make_async_copy(part, out.at[c, :, columns_of(head, width)], sems.at[at])
        for at, (c, head, part) in enumerate(sources)
    ])
    rows, columns = mine.shape[1:]
    for m, master in enumerate(masters):
        total = sum(norm[m, 0:1, 0:1] for norm in norms)
        factor = lax.rsqrt(total / (4 * rows * columns) + 1e-06) / math.sqrt(columns)
        fresh_s[m] = root_mean(mine[m] + share[m] * factor, columns)
        copies += start_all([pltpu.make_async_copy(fresh_s.at[m], master, sems.at[8 + m])])
    for copy in copies:
        copy.wait()


def call(kernel, ids, args, outs, scratch=(), far_args=False, far_outs=False, limit=16):
    given, taken = (HBM if far else VMEM for far in (far_args, far_outs))
    space = pltpu.HBM if far_args else pltpu.VMEM
    args = [pltpu.with_memory_space_constraint(a, space) for a in args]
    if not far_outs:
        outs = jax.tree.map(lambda o: pltpu.VMEM(o.shape, o.dtype), outs)
    return pl.pallas_call(
        kernel,
        out_shape=outs,
        in_specs=[SMEM] + [given] * len(args),
        out_specs=jax.tree.map(lambda _: taken, outs),
        scratch_shapes=scratch,
        compiler_params=pltpu.CompilerParams(vmem_limit_bytes=limit << 20),
    )(ids, *args)


def fast_device(query_rows, key_rows, value_rows, step_rates, gate_weight, up_weight, down_weight):
    spans, count, total_width = query_rows.shape
    heads = step_rates.shape[2]
    width = total_width // heads
    groups = lax.axis_size("ctx") // heads
    position = lax.axis_index("ctx")
    plane = position // groups
    shifts = (2, 3, 1)
    ids = jnp.stack([position & 1, position >> 1 & 1, plane] + [plane ^ s for s in shifts]).astype(jnp.int32)
    rows = gate_weight.shape[0]
    size = groups * rows
    slab = shape_of((count, width), BF16)
    two = shape_of((2, count, width), BF16)
    whole = (3, size, width)
    half = (3, 2, rows, width)
    part = (3, rows, width)
    tokens = (pltpu.VMEM((heads * count, width), BF16),) * 2

    def pair(c):
        scratch = (
            pltpu.VMEM((heads, count, width), BF16),
            pltpu.VMEM((2 * heads, count), F32),
            pltpu.SemaphoreType.DMA((3, heads)),
        )
        arrays = (key_rows, value_rows, step_rates.transpose(0, 2, 1))
        return call(functools.partial(pack_pairs, c), ids, arrays, (two,) * heads, scratch, True)

    def spread(parts):
        return [parts[0]] + [swap(parts[at + 1], s * groups) for at, s in enumerate(shifts)]

    pairs = [spread(pair(c)) for c in range(spans)]
    own, own_low = call(
        pack_own, ids, (gate_weight, up_weight, down_weight), (shape_of(part, F32), shape_of(part, BF16)),
        (pltpu.SemaphoreType.DMA((3,)),), True,
    )
    top = swap(own, 2)
    low = swap(own, 1)
    both = swap(top, 1)
    far_own = swap(own_low, 2 * groups)
    far_top = swap(far_own, 2)
    far_low = swap(far_own, 1)
    far_both = swap(far_top, 1)
    three = shape_of((3, count, width), BF16)
    *asked, ask_mine, ask_sent = call(
        pack_queries, ids, (query_rows,), (slab,) * 2 + (three,) * 2, (pltpu.SemaphoreType.DMA((8,)),), True
    )
    asked = [swap(slabs, s * groups) for slabs, s in zip(asked, shifts)]
    ask_theirs = swap(ask_sent, groups)

    first_weights, full, sent = call(
        first_step, ids, (*pairs[0], own, top, low, both),
        (shape_of(whole, BF16), shape_of(whole, F32), shape_of(whole, BF16)), tokens,
    )
    other = swap(sent, 1)
    near = swap(call(half_sum, ids, (full, other), shape_of(half, BF16)), 2)
    far = swap(near, 1)
    weights, mine = call(
        renew, ids, (own, top, low, both, full, other, near, far),
        (shape_of(whole, BF16), shape_of(part, F32)), (pltpu.VMEM(whole, F32),),
    )
    kept, sent = call(
        second_step, ids, (*pairs[1], weights), (shape_of(half, F32), shape_of(half, BF16)),
        tokens + (pltpu.VMEM(whole, F32),),
    )
    pair_s = (pltpu.VMEM((2 * count, width), BF16),)
    told_mine, told_sent = call(
        answer_near, ids, (ask_mine, ask_theirs, first_weights, far_own, far_top, far_low, far_both, weights),
        (three, three), pair_s + (pltpu.VMEM(whole, BF16),),
    )
    told = call(answer_far, ids, (*asked, weights), (slab,) * 2, pair_s)
    told = [swap(slabs, s * groups) for slabs, s in zip(told, shifts)]
    told += [told_mine, swap(told_sent, groups)]
    other = swap(sent, 1)
    share, sent = call(quarter_sum, ids, (kept, other), (shape_of(part, F32), shape_of(part, BF16)))
    share = share + swap(sent, 2).astype(F32)
    norm = jnp.broadcast_to(jnp.sum(share * share, axis=(1, 2))[:, None, None], (3, 8, 128))
    norms = [norm, swap(norm, 2), swap(norm, 3), swap(norm, 1)]
    return call(
        close, ids, (mine, share, *norms, *told),
        (shape_of(query_rows.shape, BF16),) + (shape_of((rows, width), F32),) * 3,
        (pltpu.VMEM(part, F32), pltpu.SemaphoreType.DMA((11,))), False, True,
    )


def plain_gradients(keys, scaled, low):
    gate, up, down = low
    first = mul(keys, gate, 1, 1)
    second = mul(keys, up, 1, 1)
    silu_first, slope = silu_parts(first)
    acts = (silu_first * second).astype(jnp.bfloat16)
    back = mul(scaled, down, 1, 0)
    d_gate = (back * second * slope).astype(jnp.bfloat16)
    d_up = (back * silu_first).astype(jnp.bfloat16)
    return jnp.stack([mul(d_gate, keys, 0, 0), mul(d_up, keys, 0, 0), mul(scaled, acts, 0, 0)])


def plain_answers(queries, low):
    gate, up, down = low
    acts = (jax.nn.silu(mul(queries, gate, 1, 1)) * mul(queries, up, 1, 1)).astype(jnp.bfloat16)
    return mul(acts, down, 1, 1).astype(jnp.bfloat16)


def pick(array, axis, index):
    return lax.dynamic_index_in_dim(array, index, axis, keepdims=False)


def refreshed(masters, grads, totals, per_head):
    columns = masters.shape[2]
    factor = lax.rsqrt(totals / (per_head * columns) + 1e-06) / math.sqrt(columns)
    stepped = masters + grads * factor[:, None, None]
    row_mean = jnp.mean(stepped * stepped, axis=2, keepdims=True)
    return stepped * lax.rsqrt(row_mean + 1e-06) / math.sqrt(columns)


def plain_device(query_rows, key_rows, value_rows, step_rates, gate_weight, up_weight, down_weight):
    spans, count, total_width = query_rows.shape
    heads = step_rates.shape[2]
    width = total_width // heads
    groups = lax.axis_size("ctx") // heads
    bits = groups.bit_length() - 1
    position = lax.axis_index("ctx")
    plane = position // groups
    side = [position >> level & 1 for level in range(bits)]
    shifts = sorted(range(1, heads), key=lambda m: -m.bit_length())

    def exchange(array):
        parts = [pick(array, array.ndim - 2, plane)]
        for shift in shifts:
            parts.append(swap(pick(array, array.ndim - 2, plane ^ shift), shift * groups))
        return parts

    keys = key_rows.reshape(spans, count, heads, width)
    queries = query_rows.reshape(spans, count, heads, width)
    values = value_rows.reshape(spans, count, heads, width).astype(jnp.float32)
    scaled = (step_rates[:, :, :, None] * values).astype(jnp.bfloat16)

    masters = jnp.stack([gate_weight, up_weight, down_weight])
    rows = masters.shape[1]
    pairs = [exchange(jnp.stack([keys[c], scaled[c]])) for c in range(spans)]
    asked = [exchange(queries[c]) for c in range(spans)]

    whole = masters[:, None]
    for level in reversed(range(bits)):
        other = swap(whole, 1 << level)
        low_first = side[level] == 0
        both = jnp.stack([jnp.where(low_first, whole, other), jnp.where(low_first, other, whole)], axis=2)
        whole = both.reshape(3, -1, rows, width)
    whole = whole.reshape(3, groups * rows, width)

    outs = []
    for c in range(spans):
        low = whole.astype(jnp.bfloat16)
        token_keys = jnp.concatenate([part[0] for part in pairs[c]])
        token_scaled = jnp.concatenate([part[1] for part in pairs[c]])
        grads = plain_gradients(token_keys, token_scaled, low)
        outs.append(plain_answers(jnp.concatenate(asked[c]), low))
        last = c == spans - 1
        share = grads.reshape((3,) + (2,) * bits + (rows, width))
        stops = range(bits) if last else range(bits - 1)
        for level in stops:
            axis = bits - level
            kept = pick(share, axis, side[level])
            sent = pick(share, axis, 1 - side[level]).astype(jnp.bfloat16)
            share = kept + swap(sent, 1 << level).astype(jnp.float32)
        if last:
            totals = jnp.sum(share * share, axis=(1, 2))
            for level in range(bits):
                totals = totals + swap(totals, 1 << level)
            own = lax.dynamic_slice_in_dim(whole, (position % groups) * rows, rows, 1)
            own = refreshed(own, share, totals, groups * rows)
        else:
            top = bits - 1
            share = share + swap(share.astype(jnp.bfloat16), 1 << top).astype(jnp.float32)
            for level in reversed(range(bits - 1)):
                axis = bits - level
                other = swap(share.astype(jnp.bfloat16), 1 << level).astype(jnp.float32)
                low_first = side[level] == 0
                share = jnp.stack([jnp.where(low_first, share, other), jnp.where(low_first, other, share)], axis=axis)
            share = share.reshape(3, groups * rows, width)
            totals = jnp.sum(share * share, axis=(1, 2))
            whole = refreshed(whole, share, totals, groups * rows)

    finished = []
    for c in range(spans):
        parts = outs[c].reshape(heads, count, width)
        result = jnp.zeros((count, heads, width), jnp.bfloat16)
        result = lax.dynamic_update_index_in_dim(result, parts[0], plane, 1)
        for at, shift in enumerate(shifts):
            back = swap(parts[at + 1], shift * groups)
            result = lax.dynamic_update_index_in_dim(result, back, plane ^ shift, 1)
        finished.append(result.reshape(count, total_width))
    return (jnp.stack(finished), own[0], own[1], own[2])


def solution(mesh):
    tokens = P(None, ("parts", "ctx"), None)
    weights = P(("parts", "ctx"), None)

    def per_device(*arrays):
        heads = arrays[3].shape[2]
        rows = arrays[4].shape[0]
        fast = heads == 4 and lax.axis_size("ctx") == 16 and rows % 16 == 0
        return (fast_device if fast else plain_device)(*arrays)

    return jax.shard_map(
        per_device,
        mesh=mesh,
        in_specs=(tokens,) * 4 + (weights,) * 3,
        out_specs=(tokens,) + (weights,) * 3,
        check_vma=False,
    )
```
